128 devices in a mesh: db: 64 (over z, y, x), mp: 2 (over core).
Axes of the slice: x: 4, y: 4, z: 4, core: 2. Of those that a mesh axis runs over, the one named last changes fastest.
Arguments:
- queries: bfloat16 [57344, 4096], P('db', 'mp'), may hold values from -600 to 600
- database: bfloat16 [2048, 128, 896], P('db', 'mp'), may hold values from -300 to 300
- neighbour_shard: int32 [896, 2], P('db'), may hold values from 0 to 63, all different within a row; in each aligned block of 14 rows (0 to 13, 14 to 27, ...) at most 2 rows name the same one
- neighbour_row: int32 [896, 2], P('db'), may hold values from 0 to 31
- w_key: bfloat16 [896, 4096], P(None, 'mp'), may hold values from -0.1875 to 0.1875
- w_value: bfloat16 [896, 4096], P(None, 'mp'), may hold values from -0.1875 to 0.1875
Outputs:
- attended: bfloat16 [57344, 4096], P('db', 'mp')
The draws below stay inside these ranges and needn't reach their ends.
Inputs may be any that keep to these rules, and one draw needn't show every extreme that they name: `neighbour_shard`: within the spans of one index of db no shard is named more than 2 times, and in every draw some shard is named exactly 2 times by some index; the 2 neighbours of a span lie in different shards.
All inputs are finite; a program needn't handle non-finite values.
Results may differ from the reference program's by a relative error of at most 0.01.
The reference program's roundings to bfloat16 on the way (of `rows`, `encoded` and `weights`) count: a program that leaves them out, or rounds other values in their place, can miss the bound.
Values may be sent and summed in bfloat16 or wider, within the bound.
A program may use at most 192 MiB of HBM per device.

```python
import math
import jax
import jax.numpy as jnp
import numpy as np
from jax import lax

D = 4096
HEADS = 32
HD = 128
E = 896
M = 64
R = 128
K = 2
CAP = 2
CH_DEV = 14
SHARD_ROWS = 32
SHARDS = 64
SPANS = 896
TOKENS = 57344
DB_ROWS = 2048
N_DB = 64


def draw_queries(key, part):
    noise_key = jax.random.fold_in(key, 0)
    base = jax.random.normal(noise_key, (TOKENS, D), jnp.float32)
    return jnp.clip(base, -6.0, 6.0).astype(jnp.bfloat16)


def draw_database(key, part):
    noise_key, row_key, col_key = jax.random.split(key, 3)
    col_scale = jnp.exp(jax.random.uniform(col_key, (E,), jnp.float32, 0.0, math.log(10.0)))
    row_scale = jnp.exp(jax.random.uniform(row_key, (DB_ROWS, R, 1), jnp.float32, 0.0, math.log(10.0)))
    base = jax.random.normal(noise_key, (DB_ROWS, R, E), jnp.float32)
    return jnp.clip(base * row_scale * col_scale, -300.0, 300.0).astype(jnp.bfloat16)


def with_ends(array, stream_key, smallest, top_value):
    index_at = [jax.random.randint(jax.random.fold_in(stream_key, axis), (), 0, length) for axis, length in enumerate(array.shape)]
    main_axis = array.shape.index(max(array.shape))
    next_to = index_at[:main_axis] + [(index_at[main_axis] + 1) % array.shape[main_axis]] + index_at[main_axis + 1:]
    return array.at[tuple(index_at)].set(smallest).at[tuple(next_to)].set(top_value)


def block_scale(own_key, shape, cuts, low, high):
    factor_of, own = 1.0, jax.random.fold_in(own_key, 6)
    for position, shards_of in cuts:
        heights = jnp.exp(jax.random.uniform(jax.random.fold_in(own, position), (shards_of,), jnp.float32, low / len(cuts), high / len(cuts)))
        factor_of = factor_of * jnp.repeat(heights, shape[position] // shards_of).reshape([-1 if axis == position else 1 for axis in range(len(shape))])
    return factor_of


def shared_out(rng, own, number, rows, number_of, top, most, lean):
    order = jax.random.permutation(rng, number_of)
    crowded, common = load_shares(number_of, rows * top, most, lean, True), load_shares(number_of, rows * top, most, lean, False)
    places = jnp.arange(number_of)

    def named(lengths, turn):
        used = int((lengths > 0).sum())
        fixed = max(1, used // 4)
        moved = fixed + (places - fixed + turn * (used - fixed)) % max(1, number_of - fixed)
        return jnp.zeros((number_of,), jnp.int32).at[order[jnp.where(places < fixed, places, moved)]].set(jnp.asarray(lengths, jnp.int32))

    lengths = jnp.where(number % 4 == 0, named(crowded, number // 4), named(common, number - number // 4 - 1))
    mixed = jax.random.permutation(jax.random.fold_in(own, 3), number_of)
    source_of, taker = mixed[0:number_of // 2 * 2:2], mixed[1:number_of // 2 * 2:2]
    room = jnp.minimum(lengths[source_of] - 1, most - lengths[taker]) // 2
    room = jnp.where((source_of == order[0]) | (taker == order[0]) | (lengths[taker] == 0), 0, jnp.maximum(room, 0))
    moved = jax.random.randint(jax.random.fold_in(own, 4), (number_of // 2,), 0, 1 << 20) % (room + 1)
    lengths = lengths.at[source_of].add(-moved).at[taker].add(moved)
    items = jnp.searchsorted(jnp.cumsum(lengths), jnp.arange(rows * top), side="right").astype(jnp.int32)
    listing = items.reshape(top, rows).T
    listing = listing[jax.random.permutation(jax.random.fold_in(own, 1), rows)]
    turn = jax.random.randint(jax.random.fold_in(own, 2), (rows, 1), 0, top)
    return jnp.take_along_axis(listing, (jnp.arange(top)[None, :] + turn) % top, axis=1)


def load_shares(amount, total, most, slope, full):
    loads = [(1 << 20) // math.isqrt(grade ** slope) + 1 for grade in range(1, amount + 1)]
    largest = most if full else min(most, max(-(-total // amount), total * loads[0] // sum(loads)))
    least = 1 if total - largest >= amount - 1 else 0
    holding, rest = [largest] + [least] * (amount - 1), total - largest - least * (amount - 1)
    while rest > 0:
        candidates = [i for i in range(1, amount) if holding[i] < largest] or [i for i in range(1, amount) if holding[i] < most]
        mass, left = sum([loads[i] for i in candidates]), rest
        for i in candidates:
            extra = min(most - holding[i], max(1, left * loads[i] // mass), rest)
            holding[i] = holding[i] + extra
            rest = rest - extra
    return np.array(holding)


def gaussian(own_key, dims, spread, reach, pieces=(), dtype=jnp.bfloat16):
    values = spread * jax.random.normal(own_key, dims, jnp.float32)
    if pieces:
        values = values * block_scale(own_key, dims, pieces, -0.22, 0.18)
    return jnp.clip(values, -reach, reach).astype(dtype)


def setup_inputs(seed: int = 0) -> dict:
    key_list = jax.random.split(jax.random.key(seed), 7)
    queries = draw_queries(jax.random.fold_in(key_list[6], 71), 0)
    database = draw_database(jax.random.fold_in(key_list[6], 71), 0)
    neighbour_shard_keys = jax.random.split(jax.random.fold_in(key_list[2], 1), SPANS // CH_DEV)
    neighbour_shard_turns = jax.random.permutation(jax.random.fold_in(key_list[2], 3), SPANS // CH_DEV)
    neighbour_shard = jax.vmap(lambda own, number: shared_out(jax.random.fold_in(key_list[2], 2), own, number, CH_DEV, SHARDS, K, CAP, 3))(neighbour_shard_keys, neighbour_shard_turns).reshape((SPANS, K))
    neighbour_row = with_ends(jax.random.randint(key_list[3], (SPANS, K), 0, SHARD_ROWS), jax.random.fold_in(key_list[3], 1), 0, SHARD_ROWS - 1).astype(jnp.int32)
    w_key = gaussian(key_list[4], (E, D), E ** -0.5, 0.1875, ((1, 2),))
    w_value = gaussian(key_list[5], (E, D), E ** -0.5, 0.1875, ((1, 2),))
    return {"queries": queries, "database": database, "neighbour_shard": neighbour_shard, "neighbour_row": neighbour_row, "w_key": w_key, "w_value": w_value}


def encode_block(query_block, index_block, database, w_key, w_value):
    gathered = database[index_block]
    as_float = gathered.astype(jnp.float32)
    inverse = lax.rsqrt(lax.optimization_barrier(jnp.mean(as_float * as_float, axis=-1, keepdims=True)) + 1e-06)
    encoded = (as_float * inverse).astype(jnp.bfloat16)
    encoded_rows = encoded.reshape(CH_DEV * K * R, E)
    key_rows = jnp.dot(encoded_rows, w_key, preferred_element_type=jnp.float32).astype(jnp.bfloat16)
    value_rows = jnp.dot(encoded_rows, w_value, preferred_element_type=jnp.float32).astype(jnp.bfloat16)
    key_rows = key_rows.reshape(CH_DEV, K * R, HEADS, HD)
    value_rows = value_rows.reshape(CH_DEV, K * R, HEADS, HD)
    grouped = query_block.reshape(CH_DEV, M, HEADS, HD)
    scores = jnp.einsum('cmhd,cnhd->chmn', grouped.astype(jnp.float32), key_rows.astype(jnp.float32), precision=lax.Precision.HIGHEST)
    scores = scores * (1.0 / math.sqrt(HD))
    weights = jax.nn.softmax(scores, axis=-1).astype(jnp.bfloat16)
    attended = jnp.einsum('chmn,cnhd->cmhd', weights.astype(jnp.float32), value_rows.astype(jnp.float32), precision=lax.Precision.HIGHEST)
    return attended.astype(jnp.bfloat16).reshape(CH_DEV * M, D)

def reference(queries, database, neighbour_shard, neighbour_row, w_key, w_value):
    index_all = (neighbour_shard * SHARD_ROWS + neighbour_row).astype(jnp.int32).reshape(N_DB, CH_DEV * K)
    query_all = queries.reshape(N_DB, CH_DEV * M, D)

    def one_block(block_pair):
        return encode_block(block_pair[0], block_pair[1], database, w_key, w_value)
    result = lax.map(one_block, (query_all, index_all))
    return result.reshape(TOKENS, D)
```

```python
import functools
import math

import jax
import jax.numpy as jnp
from jax import lax
from jax.experimental import pallas as pl
from jax.experimental.pallas import tpu as pltpu
from jax.sharding import PartitionSpec as P

MESH = pl.DeviceIdType.MESH
HD = 128
E = 896
STRIDES = (16, 4, 1)
PARTS = ((0, 256), (256, 256), (512, 384))
VARIANTS = ((24, 16, 13), (25, 20, 14), (26, 24, 16), (32, 32, 28))

SHIFTS = (4, 2, 0)
LANES = 128
RMAX = 32
f32 = jnp.float32


def iota(shape, axis):
    return lax.broadcasted_iota(jnp.int32, shape, axis)


def with_coord(n, shift, value):
    return n - (((n >> shift) & 3) << shift) + (value << shift)


def mm(a, b):
    return jnp.dot(a.astype(jnp.bfloat16), b.astype(jnp.bfloat16), preferred_element_type=f32)


def route_kernel(me_ref, g_ref, out_ref, present):
    me = me_ref[0]
    every = g_ref[...]
    named = jnp.concatenate(
        [jnp.max(every[4 * i : 4 * i + 4], axis=0, keepdims=True) for i in range(16)], axis=1
    )
    lane = iota((LANES, LANES), 1)
    sub = iota((LANES, LANES), 0)
    strict = (lane < sub).astype(f32)
    strict_block = jnp.where((lane < sub) & ((lane >> 5) == (sub >> 5)), 1.0, 0.0)
    upper = (sub < lane).astype(f32)

    def members(i):
        z, y, x = i // 4, i % 4, sub >> 5
        own = (jnp.full_like(x, z), jnp.full_like(x, y), x)
        inside = jnp.zeros((LANES, LANES), jnp.bool_)
        for p in range(3):
            a, b = own[p], own[(p + 1) % 3]
            inside = inside | ((lane >> 2 == p) & ((lane & 3) == a))
            inside = inside | ((lane >> 4 == p + 1) & ((lane & 15) == a * 4 + b))
        return inside.astype(jnp.bfloat16)

    group = jnp.concatenate([members(i) for i in range(16)], axis=0)
    totals = []
    for block in range(16):
        code = iota((LANES, 2048), 0) + block * LANES
        hit = (code == named).astype(jnp.bfloat16)
        there = (jnp.dot(hit, group, preferred_element_type=f32) > 0.5).astype(f32)
        present[block * LANES : (block + 1) * LANES, :] = there
        totals.append(jnp.concatenate(
            [jnp.sum(there[32 * q : 32 * q + 32], axis=0, keepdims=True) for q in range(4)], axis=0))
    total = jnp.concatenate(totals, axis=0)
    lane64 = iota((64, LANES), 1)
    need1 = jnp.max(jnp.where(lane64 < 12, total, 0.0))
    shard = iota((16, 64), 1)
    key = iota((16, 64), 0)
    need2 = jnp.zeros((), f32)
    need3 = jnp.zeros((), f32)
    valid_all = every >= 0
    for p in range(3):
        a, b, c = SHIFTS[p], SHIFTS[(p + 1) % 3], SHIFTS[(p + 2) % 3]
        pick = (((shard >> b) & 3) * 4 + ((shard >> c) & 3) == key).astype(f32)
        line = mm(pick, total)
        lane16 = iota((16, LANES), 1)
        need2 = jnp.maximum(need2, jnp.max(jnp.where(lane16 >> 4 == p + 1, line, 0.0)))
        for v in range(4):
            here = valid_all & (((every >> (5 + c)) & 3) == v)
            need3 = jnp.maximum(need3, jnp.max(jnp.sum(here.astype(f32), axis=1, keepdims=True)))

    rows1 = iota((32, LANES), 0)
    mine = present[pl.ds(pl.multiple_of(me * 32, 32), 32), :]
    rank0 = mm(strict[:32, :32], mine)
    table = []
    for j in range(RMAX):
        got = (rank0 == j) & (mine > 0.5) & (iota((32, LANES), 1) < 12)
        table.append(jnp.sum(jnp.where(got, rows1, 0), axis=0, keepdims=True))
    table = jnp.concatenate(table, axis=0)
    table3 = jnp.zeros((RMAX, LANES), f32)
    last = jnp.zeros((8, LANES), f32)
    row8 = iota((8, LANES), 0)
    lane8 = iota((8, LANES), 1)
    for p in range(3):
        a, b, c = SHIFTS[p], SHIFTS[(p + 1) % 3], SHIFTS[(p + 2) % 3]
        ma, mb, mc = (me >> a) & 3, (me >> b) & 3, (me >> c) & 3

        def line_of(base):
            return jnp.concatenate(
                [present[pl.ds(pl.multiple_of(with_coord(base, a, s) * 32, 32), 32), :] for s in range(4)],
                axis=0,
            )

        here = line_of(me)
        rank1 = mm(strict_block, here)
        at1 = jnp.sum(jnp.where(lane == p * 4 + ma, rank1, 0.0), axis=1, keepdims=True)
        at1 = at1 + (((ma - (iota((LANES, 1), 0) >> 5)) & 3) * 64).astype(f32)
        rank2 = mm(strict, here)
        use = (here > 0.5) & (lane >> 4 == p + 1)
        rank2 = jnp.where(use, rank2, -1.0)
        extra = []
        for j in range(RMAX):
            extra.append(jnp.sum(jnp.where(rank2 == j, at1, 0.0), axis=0, keepdims=True))
        table = table + jnp.concatenate(extra, axis=0).astype(jnp.int32)

        found = [jnp.zeros((1, LANES), f32) for _ in range(4)]
        count = [jnp.zeros((1, LANES), f32) for _ in range(4)]
        for sb in range(4):
            base = with_coord(me, b, sb)
            there = line_of(base)
            order = mm(strict, there)
            at2 = jnp.sum(jnp.where(lane == 16 + p * 16 + ma * 4 + mb, order, 0.0), axis=1, keepdims=True)
            at2 = at2 + (((mb - sb) & 3) * 64).astype(f32)
            unit = iota((LANES, 1), 0)
            code = (base - (((base >> a) & 3) << a) + ((unit >> 5) << a)) * 32 + (unit & 31)
            for d in range(4):
                asks = g_ref[pl.ds(with_coord(me, c, d), 1), :]
                same = code == asks
                found[d] = found[d] + jnp.sum(jnp.where(same, at2, 0.0), axis=0, keepdims=True)
                count[d] = count[d] + jnp.sum(same.astype(f32), axis=0, keepdims=True)
        rank3 = mm(jnp.concatenate(count + count, axis=0), upper)
        lane32 = iota((RMAX, LANES), 1)
        for d in range(4):
            take = (rank3[d : d + 1] == iota((RMAX, LANES), 0).astype(f32)) & (count[d] > 0.5)
            column = jnp.sum(jnp.where(take, found[d], 0.0), axis=1, keepdims=True)
            table3 = table3 + jnp.where(lane32 == p * 4 + d, column, 0.0)
        asks = g_ref[pl.ds(me, 1), :]
        chosen = [((asks >= 0) & (((asks >> (5 + c)) & 3) == v)).astype(f32) for v in range(4)]
        spots = mm(jnp.concatenate(chosen + chosen, axis=0), upper)
        final = jnp.zeros((1, LANES), f32)
        for v in range(4):
            final = final + chosen[v] * (spots[v : v + 1] + (((mc - v) & 3) * 64).astype(f32))
        last = last + jnp.where(row8 == p, final, 0.0)
    last = last + jnp.where((row8 == 3) & (lane8 == 0), need1, 0.0)
    last = last + jnp.where((row8 == 3) & (lane8 == 1), need2, 0.0)
    last = last + jnp.where((row8 == 3) & (lane8 == 2), need3, 0.0)
    out_ref[0:32, :] = table
    out_ref[32:64, :] = table3.astype(jnp.int32)
    out_ref[64:72, :] = last.astype(jnp.int32)


def route(me, everyone):
    return pl.pallas_call(
        route_kernel,
        out_shape=jax.ShapeDtypeStruct((72, LANES), jnp.int32),
        in_specs=[pl.BlockSpec(memory_space=pltpu.SMEM), pl.BlockSpec(memory_space=pltpu.VMEM)],
        out_specs=pl.BlockSpec(memory_space=pltpu.VMEM),
        scratch_shapes=[pltpu.VMEM((2048, LANES), f32)],
    )(me, everyone)


def along(n, stride, step):
    here = (n // stride) % 4
    return n + ((here + step) % 4 - here) * stride


def gather_kernel(mine_ref, all_ref, send, recv, keep):
    n, m = lax.axis_index("db"), lax.axis_index("mp")
    z, y, x = n // 16, (n // 4) % 4, n % 4
    barrier = pltpu.get_barrier_semaphore()
    for stride in STRIDES:
        for step in (1, 2, 3):
            pl.semaphore_signal(
                barrier, inc=1, device_id={"db": along(n, stride, step), "mp": m}, device_id_type=MESH
            )
    pl.semaphore_wait(barrier, 9)
    own = pltpu.make_async_copy(mine_ref, all_ref.at[z, y, x], keep)
    own.start()
    own.wait()
    for axis, stride in enumerate(STRIDES):
        where = [(z, y, x), (slice(None), y, x), (slice(None), slice(None), x)][axis]
        copies = []
        for step in (1, 2, 3):
            copies.append(
                pltpu.make_async_remote_copy(
                    src_ref=all_ref.at[where],
                    dst_ref=all_ref.at[where],
                    send_sem=send.at[axis, step - 1],
                    recv_sem=recv.at[axis, step - 1],
                    device_id={"db": along(n, stride, step), "mp": m},
                    device_id_type=MESH,
                )
            )
        for copy in copies:
            copy.start()
        for copy in copies:
            copy.wait()


def gather_asks(mine):
    return pl.pallas_call(
        gather_kernel,
        out_shape=jax.ShapeDtypeStruct((4, 4, 4, 1, LANES), jnp.int32),
        in_specs=[pl.BlockSpec(memory_space=pltpu.VMEM)],
        out_specs=pl.BlockSpec(memory_space=pltpu.VMEM),
        scratch_shapes=[
            pltpu.SemaphoreType.DMA((3, 3)),
            pltpu.SemaphoreType.DMA((3, 3)),
            pltpu.SemaphoreType.DMA,
        ],
        compiler_params=pltpu.CompilerParams(collective_id=0, has_side_effects=True),
    )(mine)


def fetch_kernel(caps, table, database, fetched, *scratch):
    c1, c2, c3 = caps
    stores, stages, first, second, third = [scratch[3 * i : 3 * i + 3] for i in range(5)]
    whole, send, recv, load, local_sem, pair_send, pair_recv = scratch[15:]
    n, m = lax.axis_index("db"), lax.axis_index("mp")
    loads = []
    for p, (start, width) in enumerate(PARTS):
        loads.append(pltpu.make_async_copy(database.at[:, :, start : start + width], stores[p], load.at[p]))
        loads[p].start()
    coords = (n // 16, (n // 4) % 4, n % 4)
    barrier = pltpu.get_barrier_semaphore()
    for stride in STRIDES:
        for step in (1, 2, 3):
            pl.semaphore_signal(
                barrier, inc=1, device_id={"db": along(n, stride, step), "mp": m}, device_id_type=MESH
            )
    pl.semaphore_signal(barrier, inc=1, device_id={"db": n, "mp": 1 - m}, device_id_type=MESH)
    pl.semaphore_wait(barrier, 10)

    def blend(values, p):
        return values[p % 3] + m * (values[(p + 1) % 3] - values[p % 3])

    def turn(p):
        return (p + m) % 3

    def peer(p, hop, step):
        here = blend(coords, p + hop)
        return n + ((here + step) % 4 - here) * blend(STRIDES, p + hop)

    def copy_of(p, hop, step, count, landing):
        return pltpu.make_async_remote_copy(
            src_ref=stages[p].at[step - 1, pl.ds(0, count)],
            dst_ref=landing.at[step],
            send_sem=send.at[p, hop, step - 1],
            recv_sem=recv.at[p, hop, step - 1],
            device_id={"db": peer(p, hop, step), "mp": m},
            device_id_type=MESH,
        )

    def run_hop(p, hop, count, source, landing, row, lane_of):
        for step in (2, 1, 3, 0):
            lane = lane_of(step)
            into = landing.at[0] if step == 0 else stages[p].at[step - 1]

            def move(j, carry):
                code = table[row + j, lane]
                if hop == 0:
                    into[j] = source[code]
                else:
                    into[j] = source[code // 64, code % 64]
                return carry

            lax.fori_loop(0, count, move, 0)
            if step:
                copy_of(p, hop, step, count, landing).start()

    def finish(p, hop, count, landing):
        for step in (1, 3, 2):
            copy_of(p, hop, step, count, landing).wait()

    for p in range(3):
        loads[p].wait()
        ma = blend(coords, p)
        run_hop(p, 0, c1, stores[p], first[p], 0, lambda s: turn(p) * 4 + (ma + s) % 4)
    for p in range(3):
        finish(p, 0, c1, first[p])
        ma, mb = blend(coords, p), blend(coords, p + 1)
        run_hop(p, 1, c2, first[p], second[p], 0,
                lambda s: 16 + turn(p) * 16 + ma * 4 + (mb + s) % 4)
    for p in range(3):
        finish(p, 1, c2, second[p])
        mc = blend(coords, p + 2)
        run_hop(p, 2, c3, second[p], third[p], 32, lambda s: turn(p) * 4 + (mc + s) % 4)
    for p in range(3):
        finish(p, 2, c3, third[p])
    chunks = 4
    asks = whole.shape[0]
    size = asks // chunks
    base = (n % 4) * 32
    pending = []
    for chunk in range(chunks):
        def place(j, carry):
            k = chunk * size + j
            for p, (start, width) in enumerate(PARTS):
                code = table[64 + turn(p), base + k]
                whole[k, :, start : start + width] = third[p][code // 64, code % 64]
            return carry

        lax.fori_loop(0, size, place, 0)
        part = pl.ds(chunk * size, size)
        near = pltpu.make_async_copy(whole.at[part], fetched.at[m, part], local_sem.at[chunk])
        far = pltpu.make_async_remote_copy(
            src_ref=whole.at[part],
            dst_ref=fetched.at[m, part],
            send_sem=pair_send.at[chunk],
            recv_sem=pair_recv.at[chunk],
            device_id={"db": n, "mp": 1 - m},
            device_id_type=MESH,
        )
        near.start()
        far.start()
        pending += [near, far]
    for copy in pending:
        copy.wait()


def fetch(variant, asks, table, database):
    caps = VARIANTS[variant]
    half = database.shape[1]
    rows = database.shape[0]

    def per_part(*lead):
        return [pltpu.VMEM(lead + (half, width), jnp.bfloat16) for _, width in PARTS]

    return pl.pallas_call(
        functools.partial(fetch_kernel, caps),
        out_shape=jax.ShapeDtypeStruct((2, asks, half, E), jnp.bfloat16),
        in_specs=[pl.BlockSpec(memory_space=pltpu.SMEM), pl.BlockSpec(memory_space=pl.ANY)],
        out_specs=pl.BlockSpec(memory_space=pl.ANY),
        scratch_shapes=[
            *per_part(rows),
            *per_part(3, max(caps)),
            *per_part(4, caps[0]),
            *per_part(4, caps[1]),
            *per_part(4, caps[2]),
            pltpu.VMEM((asks, half, E), jnp.bfloat16),
            pltpu.SemaphoreType.DMA((3, 3, 3)),
            pltpu.SemaphoreType.DMA((3, 3, 3)),
            pltpu.SemaphoreType.DMA((3,)),
            pltpu.SemaphoreType.DMA((4,)),
            pltpu.SemaphoreType.DMA((4,)),
            pltpu.SemaphoreType.DMA((4,)),
        ],
        compiler_params=pltpu.CompilerParams(
            collective_id=1 + variant, has_side_effects=True, vmem_limit_bytes=63 * 2**20
        ),
    )(table, database)


def attend_kernel(rows_ref, query_ref, key_ref, value_ref, out_ref, keys, values):
    spans = rows_ref.shape[1] // 2
    half = rows_ref.shape[2]
    tokens = query_ref.shape[0] // spans
    rows = rows_ref[...].reshape(-1, E).astype(f32)
    mean = jnp.sum(rows * rows, axis=1, keepdims=True) * (1.0 / E)
    encoded = (rows * lax.rsqrt(mean + 1e-06)).astype(jnp.bfloat16)
    width = keys.shape[1]
    for start in range(0, width, 512):
        cut = slice(start, start + 512)
        keys[:, cut] = jnp.dot(encoded, key_ref[:, cut], preferred_element_type=f32).astype(jnp.bfloat16)
        values[:, cut] = jnp.dot(encoded, value_ref[:, cut], preferred_element_type=f32).astype(jnp.bfloat16)
    far = spans * 2 * half
    for span in range(spans):
        near = slice(span * 2 * half, (span + 1) * 2 * half)
        away = slice(far + span * 2 * half, far + (span + 1) * 2 * half)
        for head in range(width // HD):
            cut = slice(head * HD, (head + 1) * HD)
            key = jnp.concatenate([keys[near, cut], keys[away, cut]], axis=0)
            value = jnp.concatenate([values[near, cut], values[away, cut]], axis=0)
            query = query_ref[span * tokens : (span + 1) * tokens, cut]
            score = lax.dot_general(query, key, (((1,), (1,)), ((), ())), preferred_element_type=f32)
            score = score * (1.0 / math.sqrt(HD))
            power = jnp.exp(score - jnp.max(score, axis=1, keepdims=True))
            weight = (power / jnp.sum(power, axis=1, keepdims=True)).astype(jnp.bfloat16)
            mixed = jnp.dot(weight, value, preferred_element_type=f32)
            out_ref[span * tokens : (span + 1) * tokens, cut] = mixed.astype(jnp.bfloat16)


def attend(fetched, queries, w_key, w_value, span_total):
    spans = 2
    half = fetched.shape[2]
    width = w_key.shape[1]
    tokens = queries.shape[0] // span_total
    whole = pl.BlockSpec((E, width), lambda i: (0, 0), pipeline_mode=pl.Buffered(1))
    return pl.pallas_call(
        attend_kernel,
        grid=(span_total // spans,),
        out_shape=jax.ShapeDtypeStruct(queries.shape, jnp.bfloat16),
        in_specs=[
            pl.BlockSpec((2, 2 * spans, half, E), lambda i: (0, i, 0, 0)),
            pl.BlockSpec((spans * tokens, width), lambda i: (i, 0)),
            whole,
            whole,
        ],
        out_specs=pl.BlockSpec((spans * tokens, width), lambda i: (i, 0)),
        scratch_shapes=[pltpu.VMEM((4 * spans * half, width), jnp.bfloat16)] * 2,
        compiler_params=pltpu.CompilerParams(
            dimension_semantics=("arbitrary",), vmem_limit_bytes=60 * 2**20
        ),
    )(fetched, queries, w_key, w_value)


def body(queries, database, neighbour_shard, neighbour_row, w_key, w_value):
    span_total = neighbour_shard.shape[0]
    asks = span_total * neighbour_shard.shape[1]
    me = lax.axis_index("db")
    code = (neighbour_shard * 32 + neighbour_row).reshape(1, asks)
    code = jnp.pad(code, ((0, 0), (0, 32 - asks)), constant_values=-1)
    code = jnp.tile(code, (1, 4))
    code = jnp.where(jnp.arange(LANES)[None, :] // 32 == me % 4, code, -1)
    everyone = gather_asks(code).reshape(64, LANES)
    table = route(me.reshape(1), everyone)
    needs = table[67, :3]
    fits = jnp.array([jnp.all(needs <= jnp.array(caps)) for caps in VARIANTS[:-1]])
    choice = jnp.sum(jnp.cumprod(1 - fits.astype(jnp.int32)))
    branches = [functools.partial(fetch, v, asks) for v in range(len(VARIANTS))]
    fetched = lax.switch(choice, branches, table, database)
    return attend(fetched, queries, w_key, w_value, span_total)


def solution(mesh):
    placed = (
        P("db", "mp"),
        P("db", "mp", None),
        P("db", None),
        P("db", None),
        P(None, "mp"),
        P(None, "mp"),
    )
    return jax.shard_map(body, mesh=mesh, in_specs=placed, out_specs=P("db", "mp"), check_vma=False)
```

```python
import functools
import math

import jax
import jax.numpy as jnp
from jax import lax
from jax.experimental import pallas as pl
from jax.experimental.pallas import tpu as pltpu
from jax.sharding import PartitionSpec as P

MESH = pl.DeviceIdType.MESH
HD = 128
E = 896
STRIDES = (16, 4, 1)
PARTS = ((0, 256), (256, 256), (512, 384))
VARIANTS = ((24, 16, 13), (25, 18, 14), (25, 21, 14), (26, 25, 16), (32, 32, 28))

SHIFTS = (4, 2, 0)
LANES = 128
RMAX = 32
f32 = jnp.float32


def iota(shape, axis):
    return lax.broadcasted_iota(jnp.int32, shape, axis)


def with_coord(n, shift, value):
    return n - (((n >> shift) & 3) << shift) + (value << shift)


def mm(a, b):
    return jnp.dot(a.astype(jnp.bfloat16), b.astype(jnp.bfloat16), preferred_element_type=f32)


def route_kernel(me_ref, g_ref, out_ref, present):
    me = me_ref[0]
    every = g_ref[...]
    named = jnp.concatenate(
        [jnp.max(every[4 * i : 4 * i + 4], axis=0, keepdims=True) for i in range(16)], axis=1
    )
    lane = iota((LANES, LANES), 1)
    sub = iota((LANES, LANES), 0)
    strict = (lane < sub).astype(f32)
    strict_block = jnp.where((lane < sub) & ((lane >> 5) == (sub >> 5)), 1.0, 0.0)
    upper = (sub < lane).astype(f32)

    def members(i):
        z, y, x = i // 4, i % 4, sub >> 5
        own = (jnp.full_like(x, z), jnp.full_like(x, y), x)
        inside = jnp.zeros((LANES, LANES), jnp.bool_)
        for p in range(3):
            a, b = own[p], own[(p + 1) % 3]
            inside = inside | ((lane >> 2 == p) & ((lane & 3) == a))
            inside = inside | ((lane >> 4 == p + 1) & ((lane & 15) == a * 4 + b))
        return inside.astype(jnp.bfloat16)

    group = jnp.concatenate([members(i) for i in range(16)], axis=0)
    totals = []
    for block in range(16):
        code = iota((LANES, 2048), 0) + block * LANES
        hit = (code == named).astype(jnp.bfloat16)
        there = (jnp.dot(hit, group, preferred_element_type=f32) > 0.5).astype(f32)
        present[block * LANES : (block + 1) * LANES, :] = there
        totals.append(jnp.concatenate(
            [jnp.sum(there[32 * q : 32 * q + 32], axis=0, keepdims=True) for q in range(4)], axis=0))
    total = jnp.concatenate(totals, axis=0)
    lane64 = iota((64, LANES), 1)
    need1 = jnp.max(jnp.where(lane64 < 12, total, 0.0))
    shard = iota((16, 64), 1)
    key = iota((16, 64), 0)
    need2 = jnp.zeros((), f32)
    need3 = jnp.zeros((), f32)
    valid_all = every >= 0
    for p in range(3):
        a, b, c = SHIFTS[p], SHIFTS[(p + 1) % 3], SHIFTS[(p + 2) % 3]
        pick = (((shard >> b) & 3) * 4 + ((shard >> c) & 3) == key).astype(f32)
        line = mm(pick, total)
        lane16 = iota((16, LANES), 1)
        need2 = jnp.maximum(need2, jnp.max(jnp.where(lane16 >> 4 == p + 1, line, 0.0)))
        for v in range(4):
            here = valid_all & (((every >> (5 + c)) & 3) == v)
            need3 = jnp.maximum(need3, jnp.max(jnp.sum(here.astype(f32), axis=1, keepdims=True)))

    rows1 = iota((32, LANES), 0)
    mine = present[pl.ds(pl.multiple_of(me * 32, 32), 32), :]
    rank0 = mm(strict[:32, :32], mine)
    table = []
    for j in range(RMAX):
        got = (rank0 == j) & (mine > 0.5) & (iota((32, LANES), 1) < 12)
        table.append(jnp.sum(jnp.where(got, rows1, 0), axis=0, keepdims=True))
    table = jnp.concatenate(table, axis=0)
    table3 = jnp.zeros((RMAX, LANES), f32)
    last = jnp.zeros((8, LANES), f32)
    row8 = iota((8, LANES), 0)
    lane8 = iota((8, LANES), 1)
    for p in range(3):
        a, b, c = SHIFTS[p], SHIFTS[(p + 1) % 3], SHIFTS[(p + 2) % 3]
        ma, mb, mc = (me >> a) & 3, (me >> b) & 3, (me >> c) & 3

        def line_of(base):
            return jnp.concatenate(
                [present[pl.ds(pl.multiple_of(with_coord(base, a, s) * 32, 32), 32), :] for s in range(4)],
                axis=0,
            )

        here = line_of(me)
        rank1 = mm(strict_block, here)
        at1 = jnp.sum(jnp.where(lane == p * 4 + ma, rank1, 0.0), axis=1, keepdims=True)
        at1 = at1 + (((ma - (iota((LANES, 1), 0) >> 5)) & 3) * 64).astype(f32)
        rank2 = mm(strict, here)
        use = (here > 0.5) & (lane >> 4 == p + 1)
        rank2 = jnp.where(use, rank2, -1.0)
        extra = []
        for j in range(RMAX):
            extra.append(jnp.sum(jnp.where(rank2 == j, at1, 0.0), axis=0, keepdims=True))
        table = table + jnp.concatenate(extra, axis=0).astype(jnp.int32)

        found = [jnp.zeros((1, LANES), f32) for _ in range(4)]
        count = [jnp.zeros((1, LANES), f32) for _ in range(4)]
        for sb in range(4):
            base = with_coord(me, b, sb)
            there = line_of(base)
            order = mm(strict, there)
            at2 = jnp.sum(jnp.where(lane == 16 + p * 16 + ma * 4 + mb, order, 0.0), axis=1, keepdims=True)
            at2 = at2 + (((mb - sb) & 3) * 64).astype(f32)
            unit = iota((LANES, 1), 0)
            code = (base - (((base >> a) & 3) << a) + ((unit >> 5) << a)) * 32 + (unit & 31)
            for d in range(4):
                asks = g_ref[pl.ds(with_coord(me, c, d), 1), :]
                same = code == asks
                found[d] = found[d] + jnp.sum(jnp.where(same, at2, 0.0), axis=0, keepdims=True)
                count[d] = count[d] + jnp.sum(same.astype(f32), axis=0, keepdims=True)
        rank3 = mm(jnp.concatenate(count + count, axis=0), upper)
        lane32 = iota((RMAX, LANES), 1)
        for d in range(4):
            take = (rank3[d : d + 1] == iota((RMAX, LANES), 0).astype(f32)) & (count[d] > 0.5)
            column = jnp.sum(jnp.where(take, found[d], 0.0), axis=1, keepdims=True)
            table3 = table3 + jnp.where(lane32 == p * 4 + d, column, 0.0)
        asks = g_ref[pl.ds(me, 1), :]
        chosen = [((asks >= 0) & (((asks >> (5 + c)) & 3) == v)).astype(f32) for v in range(4)]
        spots = mm(jnp.concatenate(chosen + chosen, axis=0), upper)
        final = jnp.zeros((1, LANES), f32)
        for v in range(4):
            final = final + chosen[v] * (spots[v : v + 1] + (((mc - v) & 3) * 64).astype(f32))
        last = last + jnp.where(row8 == p, final, 0.0)
    last = last + jnp.where((row8 == 3) & (lane8 == 0), need1, 0.0)
    last = last + jnp.where((row8 == 3) & (lane8 == 1), need2, 0.0)
    last = last + jnp.where((row8 == 3) & (lane8 == 2), need3, 0.0)
    choice = jnp.zeros((), jnp.int32)
    fits = jnp.zeros((), jnp.bool_)
    for caps in VARIANTS[:-1]:
        fits = fits | ((need1 <= caps[0]) & (need2 <= caps[1]) & (need3 <= caps[2]))
        choice = choice + jnp.where(fits, 0, 1)
    last = last + jnp.where((row8 == 3) & (lane8 == 3), choice.astype(f32), 0.0)
    out_ref[0:32, :] = table
    out_ref[32:64, :] = table3.astype(jnp.int32)
    out_ref[64:72, :] = last.astype(jnp.int32)


def route(me, everyone):
    return pl.pallas_call(
        route_kernel,
        out_shape=jax.ShapeDtypeStruct((72, LANES), jnp.int32),
        in_specs=[pl.BlockSpec(memory_space=pltpu.SMEM), pl.BlockSpec(memory_space=pltpu.VMEM)],
        out_specs=pl.BlockSpec(memory_space=pltpu.VMEM),
        scratch_shapes=[pltpu.VMEM((2048, LANES), f32)],
    )(me, everyone)


def along(n, stride, step):
    here = (n // stride) % 4
    return n + ((here + step) % 4 - here) * stride


def gather_kernel(mine_ref, all_ref, send, recv, keep):
    n, m = lax.axis_index("db"), lax.axis_index("mp")
    z, y, x = n // 16, (n // 4) % 4, n % 4
    barrier = pltpu.get_barrier_semaphore()
    for stride in STRIDES:
        for step in (1, 2, 3):
            pl.semaphore_signal(
                barrier, inc=1, device_id={"db": along(n, stride, step), "mp": m}, device_id_type=MESH
            )
    pl.semaphore_wait(barrier, 9)
    own = pltpu.make_async_copy(mine_ref, all_ref.at[z, y, x], keep)
    own.start()
    own.wait()
    for axis, stride in enumerate(STRIDES):
        where = [(z, y, x), (slice(None), y, x), (slice(None), slice(None), x)][axis]
        copies = []
        for step in (1, 2, 3):
            copies.append(
                pltpu.make_async_remote_copy(
                    src_ref=all_ref.at[where],
                    dst_ref=all_ref.at[where],
                    send_sem=send.at[axis, step - 1],
                    recv_sem=recv.at[axis, step - 1],
                    device_id={"db": along(n, stride, step), "mp": m},
                    device_id_type=MESH,
                )
            )
        for copy in copies:
            copy.start()
        for copy in copies:
            copy.wait()


def gather_asks(mine):
    return pl.pallas_call(
        gather_kernel,
        out_shape=jax.ShapeDtypeStruct((4, 4, 4, 1, LANES), jnp.int32),
        in_specs=[pl.BlockSpec(memory_space=pltpu.VMEM)],
        out_specs=pl.BlockSpec(memory_space=pltpu.VMEM),
        scratch_shapes=[
            pltpu.SemaphoreType.DMA((3, 3)),
            pltpu.SemaphoreType.DMA((3, 3)),
            pltpu.SemaphoreType.DMA,
        ],
        compiler_params=pltpu.CompilerParams(collective_id=0, has_side_effects=True),
    )(mine)


def fetch_kernel(caps, table, database, fetched, *scratch):
    c1, c2, c3 = caps
    stores, stages, first, second, third = [scratch[3 * i : 3 * i + 3] for i in range(5)]
    whole, send, recv, load, local_sem, pair_send, pair_recv = scratch[15:]
    n, m = lax.axis_index("db"), lax.axis_index("mp")
    loads = []
    for p, (start, width) in enumerate(PARTS):
        loads.append(pltpu.make_async_copy(database.at[:, :, start : start + width], stores[p], load.at[p]))
        loads[p].start()
    coords = (n // 16, (n // 4) % 4, n % 4)
    barrier = pltpu.get_barrier_semaphore()
    for stride in STRIDES:
        for step in (1, 2, 3):
            pl.semaphore_signal(
                barrier, inc=1, device_id={"db": along(n, stride, step), "mp": m}, device_id_type=MESH
            )
    pl.semaphore_signal(barrier, inc=1, device_id={"db": n, "mp": 1 - m}, device_id_type=MESH)
    pl.semaphore_wait(barrier, 10)

    def blend(values, p):
        return values[p % 3] + m * (values[(p + 1) % 3] - values[p % 3])

    def turn(p):
        return (p + m) % 3

    def peer(p, hop, step):
        here = blend(coords, p + hop)
        return n + ((here + step) % 4 - here) * blend(STRIDES, p + hop)

    def copy_of(p, hop, step, count, landing):
        return pltpu.make_async_remote_copy(
            src_ref=stages[p].at[step - 1, pl.ds(0, count)],
            dst_ref=landing.at[step],
            send_sem=send.at[p, hop, step - 1],
            recv_sem=recv.at[p, hop, step - 1],
            device_id={"db": peer(p, hop, step), "mp": m},
            device_id_type=MESH,
        )

    def run_hop(p, hop, count, source, landing, row, lane_of):
        for step in (2, 1, 3, 0):
            lane = lane_of(step)
            into = landing.at[0] if step == 0 else stages[p].at[step - 1]

            def move(j, carry):
                code = table[row + j, lane]
                if hop == 0:
                    into[j] = source[code]
                else:
                    into[j] = source[code // 64, code % 64]
                return carry

            lax.fori_loop(0, count, move, 0)
            if step:
                copy_of(p, hop, step, count, landing).start()

    def finish(p, hop, count, landing):
        for step in (1, 3, 2):
            copy_of(p, hop, step, count, landing).wait()

    for p in range(3):
        loads[p].wait()
        ma = blend(coords, p)
        run_hop(p, 0, c1, stores[p], first[p], 0, lambda s: turn(p) * 4 + (ma + s) % 4)
    for p in range(3):
        finish(p, 0, c1, first[p])
        ma, mb = blend(coords, p), blend(coords, p + 1)
        run_hop(p, 1, c2, first[p], second[p], 0,
                lambda s: 16 + turn(p) * 16 + ma * 4 + (mb + s) % 4)
    for p in range(3):
        finish(p, 1, c2, second[p])
        mc = blend(coords, p + 2)
        run_hop(p, 2, c3, second[p], third[p], 32, lambda s: turn(p) * 4 + (mc + s) % 4)
    for p in range(3):
        finish(p, 2, c3, third[p])
    chunks = 4
    asks = whole.shape[0]
    size = asks // chunks
    base = (n % 4) * 32
    pending = []
    for chunk in range(chunks):
        def place(j, carry):
            k = chunk * size + j
            for p, (start, width) in enumerate(PARTS):
                code = table[64 + turn(p), base + k]
                whole[k, :, start : start + width] = third[p][code // 64, code % 64]
            return carry

        lax.fori_loop(0, size, place, 0)
        part = pl.ds(chunk * size, size)
        near = pltpu.make_async_copy(whole.at[part], fetched.at[m, part], local_sem.at[chunk])
        far = pltpu.make_async_remote_copy(
            src_ref=whole.at[part],
            dst_ref=fetched.at[m, part],
            send_sem=pair_send.at[chunk],
            recv_sem=pair_recv.at[chunk],
            device_id={"db": n, "mp": 1 - m},
            device_id_type=MESH,
        )
        near.start()
        far.start()
        pending += [near, far]
    for copy in pending:
        copy.wait()


def fetch(variant, asks, table, database):
    caps = VARIANTS[variant]
    half = database.shape[1]
    rows = database.shape[0]

    def per_part(*lead):
        return [pltpu.VMEM(lead + (half, width), jnp.bfloat16) for _, width in PARTS]

    return pl.pallas_call(
        functools.partial(fetch_kernel, caps),
        out_shape=jax.ShapeDtypeStruct((2, asks, half, E), jnp.bfloat16),
        in_specs=[pl.BlockSpec(memory_space=pltpu.SMEM), pl.BlockSpec(memory_space=pl.ANY)],
        out_specs=pl.BlockSpec(memory_space=pl.ANY),
        scratch_shapes=[
            *per_part(rows),
            *per_part(3, max(caps)),
            *per_part(4, caps[0]),
            *per_part(4, caps[1]),
            *per_part(4, caps[2]),
            pltpu.VMEM((asks, half, E), jnp.bfloat16),
            pltpu.SemaphoreType.DMA((3, 3, 3)),
            pltpu.SemaphoreType.DMA((3, 3, 3)),
            pltpu.SemaphoreType.DMA((3,)),
            pltpu.SemaphoreType.DMA((4,)),
            pltpu.SemaphoreType.DMA((4,)),
            pltpu.SemaphoreType.DMA((4,)),
        ],
        compiler_params=pltpu.CompilerParams(
            collective_id=1 + variant, has_side_effects=True, vmem_limit_bytes=63 * 2**20
        ),
    )(table, database)


def attend_kernel(rows_ref, query_ref, key_ref, value_ref, out_ref, keys, values):
    step, last = pl.program_id(0), pl.num_programs(0) - 1
    tokens, width = query_ref.shape
    pairs = width // (2 * HD)
    factor = math.log2(math.e) / math.sqrt(HD)
    blank = jnp.zeros((tokens, HD), jnp.bfloat16)

    def run(project, attending):
        new = step % 2
        old = 1 - new
        if project:
            rows = rows_ref[...].reshape(-1, E).astype(f32)
            mean = jnp.sum(rows * rows, axis=1, keepdims=True) * (1.0 / E)
            encoded = (rows * lax.rsqrt(mean + 1e-06)).astype(jnp.bfloat16)

        def score_of(pair):
            cut = slice(pair * 2 * HD, (pair + 1) * 2 * HD)
            query = query_ref[:, cut]
            left = jnp.concatenate([query[:, :HD], blank], axis=1)
            right = jnp.concatenate([blank, query[:, HD:]], axis=1)
            both = jnp.concatenate([left, right], axis=0)
            return lax.dot_general(
                both, keys[old, :, cut], (((1,), (1,)), ((), ())), preferred_element_type=f32
            )

        def softmax(score):
            power = jnp.exp2((score - jnp.max(score, axis=1, keepdims=True)) * factor)
            return (power * (1.0 / jnp.sum(power, axis=1, keepdims=True))).astype(jnp.bfloat16)

        def mix(pair, weight):
            cut = slice(pair * 2 * HD, (pair + 1) * 2 * HD)
            mixed = jnp.dot(weight, values[old, :, cut], preferred_element_type=f32)
            mixed = jnp.concatenate([mixed[:tokens, :HD], mixed[tokens:, HD:]], axis=1)
            out_ref[:, cut] = mixed.astype(jnp.bfloat16)

        score = score_of(0) if attending else None
        held = None
        for pair in range(pairs):
            cut = slice(pair * 2 * HD, (pair + 1) * 2 * HD)
            if attending:
                ahead = score_of(pair + 1) if pair + 1 < pairs else None
                weight = softmax(score)
            if project:
                keys[new, :, cut] = jnp.dot(
                    encoded, key_ref[:, cut], preferred_element_type=f32
                ).astype(jnp.bfloat16)
                values[new, :, cut] = jnp.dot(
                    encoded, value_ref[:, cut], preferred_element_type=f32
                ).astype(jnp.bfloat16)
            if attending:
                if pair:
                    mix(pair - 1, held)
                held, score = weight, ahead
        if attending:
            mix(pairs - 1, held)

    @pl.when(step == 0)
    def _():
        run(True, False)

    @pl.when((step > 0) & (step < last))
    def _():
        run(True, True)

    @pl.when(step == last)
    def _():
        run(False, True)


def attend(fetched, queries, w_key, w_value, span_total):
    half = fetched.shape[2]
    width = w_key.shape[1]
    tokens = queries.shape[0] // span_total
    whole = pl.BlockSpec((E, width), lambda i: (0, 0), pipeline_mode=pl.Buffered(1))
    behind = pl.BlockSpec((tokens, width), lambda i: (jnp.maximum(i - 1, 0), 0))
    return pl.pallas_call(
        attend_kernel,
        grid=(span_total + 1,),
        out_shape=jax.ShapeDtypeStruct(queries.shape, jnp.bfloat16),
        in_specs=[
            pl.BlockSpec((2, 2, half, E), lambda i: (0, jnp.minimum(i, span_total - 1), 0, 0)),
            behind,
            whole,
            whole,
        ],
        out_specs=behind,
        scratch_shapes=[pltpu.VMEM((2, 4 * half, width), jnp.bfloat16)] * 2,
        compiler_params=pltpu.CompilerParams(
            dimension_semantics=("arbitrary",), vmem_limit_bytes=60 * 2**20
        ),
    )(fetched, queries, w_key, w_value)


def body(queries, database, neighbour_shard, neighbour_row, w_key, w_value):
    span_total = neighbour_shard.shape[0]
    asks = span_total * neighbour_shard.shape[1]
    me = lax.axis_index("db")
    code = (neighbour_shard * 32 + neighbour_row).reshape(1, asks)
    code = jnp.pad(code, ((0, 0), (0, 32 - asks)), constant_values=-1)
    code = jnp.tile(code, (1, 4))
    code = jnp.where(jnp.arange(LANES)[None, :] // 32 == me % 4, code, -1)
    everyone = gather_asks(code).reshape(64, LANES)
    table = route(me.reshape(1), everyone)
    branches = [functools.partial(fetch, v, asks) for v in range(len(VARIANTS))]
    fetched = lax.switch(table[67, 3], branches, table, database)
    return attend(fetched, queries, w_key, w_value, span_total)


def solution(mesh):
    placed = (
        P("db", "mp"),
        P("db", "mp", None),
        P("db", None),
        P("db", None),
        P(None, "mp"),
        P(None, "mp"),
    )
    return jax.shard_map(body, mesh=mesh, in_specs=placed, out_specs=P("db", "mp"), check_vma=False)
```
